512 devices in a mesh: sec: 32 (over z, core), blk: 16 (over y, x).
Axes of the slice: x: 4, y: 4, z: 16, core: 2. Of those that a mesh axis runs over, the one named last changes fastest.
Arguments:
- left_env: bfloat16 [32, 14, 16, 256, 256], P('sec', None, 'blk'), may hold values from -0.375 to 0.375
- right_out: bfloat16 [32, 14, 16, 256, 256], P('sec', None, 'blk'), may hold values from -0.09375 to 0.09375
- onsite: bfloat16 [32, 16, 256, 256], P('sec', 'blk'), may hold values from -1 to 1
- start_state: float32 [32, 16, 256, 256], P('sec', 'blk'), may hold values from -40 to 40
- live: int32 [32, 16], P('sec', 'blk'), may hold values from 64 to 256, as said below
- rank: int32 [32, 16], P('sec', 'blk'), may hold values from 1 to 256, as said below
- shift: int32 [14], replicated, may hold values from -1 to 1
Outputs:
- theta_out: float32 [32, 16, 256, 256], P('sec', 'blk')
- energies: float32 [32], P('sec')
- density: float32 [32, 16, 256, 256], P('sec', 'blk')
The draws below stay inside these ranges and needn't reach their ends.
Inputs may be any that keep to these rules, and one draw needn't show every extreme that they name: live rows of a padded block; the middle block 8 of every section is full. Kept rank of a block, never more than its live rows; the middle block of every section keeps all 256.
All inputs are finite; a program needn't handle non-finite values.
Results may differ from the reference program's by a relative error of at most 0.003.
Values may be sent and summed in bfloat16 or wider, within the bound.
No kernel may reach another device: no remote copies, remote signals or barrier semaphores. Data moves between devices by JAX's collectives and lax.ppermute only.
A program may use at most 64 MiB of HBM per device.

```python
import jax
import jax.numpy as jnp
from jax import lax

BS = 256
K = 14
NB_DEV = 1
ITERS = 3
NB = 16
NSEC = 32


def live_and_rank(key):
    base = jax.random.fold_in(key, 17)
    first_key, second_key = jax.random.split(base)
    live_rows = jax.random.randint(first_key, (NSEC, NB), BS // 4, BS + 1)
    live_rows = live_rows.at[:, NB // 2].set(BS)
    kept = jax.random.randint(second_key, (NSEC, NB), 1, live_rows + 1)
    kept = kept.at[:, NB // 2].set(BS)
    return (live_rows.astype(jnp.int32), kept.astype(jnp.int32))


def draw_live(key, part):
    return live_and_rank(key)[0]


def draw_rank(key, part):
    return live_and_rank(key)[1]


def draw_start_state(key, part):
    first_key = jax.random.fold_in(jax.random.fold_in(key, 5), 0)
    ramp = 1.0 + 2.0 * jnp.arange(NB, dtype=jnp.float32) / (NB - 1)
    values = jax.random.normal(first_key, (NSEC, NB, BS, BS), jnp.float32)
    values = values * ramp[None, :, None, None]
    return jnp.clip(values, -40.0, 40.0).astype(jnp.float32)


def draw_onsite(key, part):
    first_key, second_key = jax.random.split(jax.random.fold_in(key, 29))
    spread = 1.0 / jnp.sqrt(jnp.float32(BS))
    values = jax.random.normal(first_key, (NSEC, NB, BS, BS), jnp.float32) * spread
    level = jax.random.uniform(second_key, (NSEC, NB, 1, 1), jnp.float32, 0.2, 0.4)
    rows = jnp.arange(BS, dtype=jnp.int32)
    diagonal = (rows[:, None] == rows[None, :]).astype(jnp.float32)
    values = values + level * diagonal[None, None, :, :]
    return jnp.clip(values, -1.0, 1.0).astype(jnp.bfloat16)


def with_ends(drawn, own_key, least, top_value):
    index_at = [jax.random.randint(jax.random.fold_in(own_key, axis), (), 0, length) for axis, length in enumerate(drawn.shape)]
    longest = drawn.shape.index(max(drawn.shape))
    next_to = index_at[:longest] + [(index_at[longest] + 1) % drawn.shape[longest]] + index_at[longest + 1:]
    return drawn.at[tuple(index_at)].set(least).at[tuple(next_to)].set(top_value)


def shard_levels(rng, shape, cuts, smallest, top_value):
    factor_of = 1.0
    for position, parts in cuts:
        steps = jax.random.uniform(jax.random.fold_in(jax.random.fold_in(rng, 6), position), (parts,), jnp.float32, smallest / len(cuts), top_value / len(cuts))
        factor_of = factor_of * jnp.repeat(jnp.exp(steps), shape[position] // parts).reshape((-1,) + (1,) * (len(shape) - 1 - position))
    return factor_of


def gaussian(own_key, dims, deviation, reach, shards=(), held_as=jnp.bfloat16):
    gain = shard_levels(own_key, dims, shards, -0.22, 0.18) if shards else 1.0
    drawn = jax.random.normal(own_key, dims, jnp.float32) * deviation * gain
    return jnp.minimum(jnp.maximum(drawn, -reach), reach).astype(held_as)


def setup_inputs(seed: int = 0) -> dict:
    arg_keys = jax.random.split(jax.random.key(seed), 8)
    return {
        "left_env": gaussian(arg_keys[0], (NSEC, K, NB, BS, BS), BS ** -0.5, 0.375, ((0, 32), (2, 16))),
        "right_out": gaussian(arg_keys[1], (NSEC, K, NB, BS, BS), (BS * K) ** -0.5, 0.09375, ((0, 32), (2, 16))),
        "onsite": draw_onsite(jax.random.fold_in(arg_keys[7], 71), 0),
        "start_state": draw_start_state(jax.random.fold_in(arg_keys[7], 71), 0),
        "live": draw_live(jax.random.fold_in(arg_keys[7], 71), 0),
        "rank": draw_rank(jax.random.fold_in(arg_keys[7], 71), 0),
        "shift": with_ends(jax.random.randint(arg_keys[6], (K,), 0 - NB_DEV, NB_DEV + 1), jax.random.fold_in(arg_keys[6], 1), 0 - NB_DEV, NB_DEV).astype(jnp.int32),
    }


def apply_block(left_blocks, right_blocks, onsite_blocks, state_half, cell_mask, shift):
    count = state_half.shape[0]
    target = jnp.arange(count, dtype=jnp.int32)[None, :] + shift[:, None]
    usable = ((target >= 0) & (target < count)).astype(jnp.float32)
    state_full = state_half.astype(jnp.float32)
    picked = state_full[jnp.clip(target, 0, count - 1)] * usable[:, :, None, None]
    inner = jnp.einsum('kbij,kbjl->kbil', left_blocks.astype(jnp.float32), picked).astype(jnp.bfloat16)
    applied = jnp.einsum('kbil,kbml->bim', inner.astype(jnp.float32), right_blocks.astype(jnp.float32))
    onsite_full = onsite_blocks.astype(jnp.float32)
    applied = applied + jnp.einsum('bij,bjl->bil', onsite_full, state_full)
    applied = applied + jnp.einsum('bil,bml->bim', state_full, onsite_full)
    return applied * cell_mask

def reference(left_env, right_out, onsite, start_state, live, rank, shift):
    positions = jnp.arange(BS, dtype=jnp.int32)

    def one_section(section):
        following = jnp.minimum(section + 1, NSEC - 1)
        present = (section + 1 < NSEC).astype(jnp.bfloat16)
        right_blocks = right_out[following] * present
        left_blocks = left_env[section]
        onsite_blocks = onsite[section]
        inside = positions[None, :] < live[section][:, None]
        cell_mask = (inside[:, :, None] & inside[:, None, :]).astype(jnp.float32)
        state = start_state[section] * cell_mask
        energy = jnp.zeros((), jnp.float32)
        for iteration in range(ITERS):
            state_half = state.astype(jnp.bfloat16)
            applied = apply_block(left_blocks, right_blocks, onsite_blocks, state_half, cell_mask, shift)
            correlation = jnp.sum(state * applied)
            weight = jnp.sum(state * state)
            energy = correlation / weight
            resid = applied - energy * state
            resid_norm = jnp.sum(resid * resid)
            state = (state - 0.3 * resid) / jnp.sqrt(1.0 + 0.09 * resid_norm / weight)
        return (state, energy)
    theta_out, energies = lax.map(one_section, jnp.arange(NSEC, dtype=jnp.int32))
    final_half = theta_out.astype(jnp.bfloat16)
    beside = jnp.concatenate([final_half[1:], jnp.zeros_like(final_half[:1])], axis=0)
    keep = (positions[None, None, :] < rank[:, :, None]).astype(jnp.bfloat16)
    own_part = jnp.einsum('sbij,sbmj->sbim', (final_half * keep[:, :, None, :]).astype(jnp.float32), final_half.astype(jnp.float32))
    other_part = jnp.einsum('sbji,sbjm->sbim', (beside * keep[:, :, :, None]).astype(jnp.float32), beside.astype(jnp.float32))
    return (theta_out, energies, own_part + other_part)
```

```python
import functools

import jax
import jax.numpy as jnp
from jax import lax
from jax.experimental import pallas as pl
from jax.experimental.pallas import tpu as pltpu
from jax.sharding import PartitionSpec as P

STEP = 0.3
VM = pl.BlockSpec(memory_space=pltpu.VMEM)
SM = pl.BlockSpec(memory_space=pltpu.SMEM)
F32 = jnp.float32
BF = jnp.bfloat16
LIMIT = 20 * 1024 * 1024


def call(body, outs, args, specs, scratch=(), flops=10**8, out_specs=None):
    moved = sum(a.size * a.dtype.itemsize for a in args)
    return pl.pallas_call(
        body,
        out_shape=[jax.ShapeDtypeStruct(s, d) for s, d in outs],
        in_specs=specs,
        out_specs=out_specs or [VM] * len(outs),
        scratch_shapes=list(scratch),
        compiler_params=pltpu.CompilerParams(vmem_limit_bytes=LIMIT),
        cost_estimate=pl.CostEstimate(flops=flops, bytes_accessed=moved, transcendentals=0),
    )(*args)


def dot(a, b):
    return jnp.dot(a, b, preferred_element_type=F32)


def dot_t(a, b):
    return lax.dot_general(a, b, (((1,), (1,)), ((), ())), preferred_element_type=F32)


def inside(live, shape):
    rows = lax.broadcasted_iota(jnp.int32, shape, 0)
    cols = lax.broadcasted_iota(jnp.int32, shape, 1)
    return (rows < live) & (cols < live)


def init_body(live, start, p_ref, h_ref):
    p = jnp.where(inside(live[0, 0], start.shape), start[...], 0.0)
    p_ref[...] = p
    h_ref[...] = p.astype(BF)


def fill(hs, before, own, after):
    hs[0] = before[...]
    hs[1] = own[...]
    hs[2] = after[...]


def inner_body(shift, left, before, own, after, onsite, inner, total, hs):
    fill(hs, before, own, after)
    h = own[...]
    total[...] = dot(onsite[...], h) + dot_t(h, onsite[...])
    for k in range(left.shape[0]):
        inner[k] = dot(left[k], hs[shift[k] + 1]).astype(BF)


def finish(total, live, p, w_ref, p_ref, h_ref):
    w = jnp.where(inside(live, total.shape), total, 0.0)
    w_ref[...] = w
    q = p - STEP * w
    p_ref[...] = q
    h_ref[...] = q.astype(BF)
    return w, q


def outer_body(live, inner, right, start, p, w_ref, p_ref, h_ref):
    total = start[...]
    for k in range(right.shape[0]):
        total = total + dot_t(inner[k], right[k])
    finish(total, live[0, 0], p[...], w_ref, p_ref, h_ref)


def both_body(shift, live, left, right, before, own, after, onsite, p, w_ref, p_ref, h_ref, hs):
    fill(hs, before, own, after)
    h = own[...]
    total = dot(onsite[...], h) + dot_t(h, onsite[...])
    for k in range(left.shape[0]):
        part = dot(left[k], hs[shift[k] + 1]).astype(BF)
        total = total + dot_t(part, right[k])
    finish(total, live[0, 0], p[...], w_ref, p_ref, h_ref)


def gram_body(p0, w0, w1, w2, g_ref):
    a, b, c, d = p0[...], w0[...], w1[...], w2[...]
    pairs = ((a, a), (a, b), (a, c), (a, d), (b, b), (b, c), (b, d), (c, c), (c, d), (d, d))
    lane = lax.broadcasted_iota(jnp.int32, g_ref.shape, 1)
    out = jnp.zeros(g_ref.shape, F32)
    for i, (x, y) in enumerate(pairs):
        out = jnp.where(lane == i, jnp.sum(x * y), out)
    g_ref[...] = out


def final_body(parts, p0, p1, p2, p3, theta_ref, half_ref, energy_ref):
    sums = jnp.sum(parts[...], axis=0, keepdims=True)
    v = [sums[:, i : i + 1] for i in range(10)]
    weight, p0w = v[0], [v[1], v[2], v[3]]
    ww = [[v[4], v[5], v[6]], [v[5], v[7], v[8]], [v[6], v[8], v[9]]]
    p1w = [p0w[j] - STEP * ww[0][j] for j in range(3)]
    p2w = [p1w[j] - STEP * ww[1][j] for j in range(3)]
    pw = [p0w, p1w, p2w]
    one = jnp.ones_like(weight)
    coef, scale = [one], one
    energy = one
    for n in range(3):
        c = jnp.zeros_like(one)
        a = jnp.zeros_like(one)
        for i in range(n + 1):
            for j in range(n + 1):
                t = coef[i] * coef[j]
                c = c + t * pw[i][j]
                a = a + t * ww[i][j]
        energy = c * scale / weight
        excess = jnp.maximum(a * scale / weight - energy * energy, 0.0)
        scale = scale / (1.0 + STEP * STEP * excess)
        g = STEP * energy
        coef = [g * coef[0]] + [coef[i - 1] + g * coef[i] for i in range(1, n + 1)] + [one]
    energy_ref[...] = jnp.broadcast_to(energy, energy_ref.shape)
    root = jnp.sqrt(scale)
    theta = (root * coef[0]) * p0[...] + (root * coef[1]) * p1[...]
    theta = theta + (root * coef[2]) * p2[...] + root * p3[...]
    theta_ref[...] = theta
    half_ref[...] = theta.astype(BF)


def per_device(left_env, right_out, onsite, start_state, live, rank, shift):
    terms, width = left_env.shape[1], left_env.shape[-1]
    square = (width, width)
    left = left_env.reshape(terms, *square)
    onsite = onsite.reshape(square)
    sections, blocks = lax.axis_size("sec"), lax.axis_size("blk")
    ahead = [(i + 1, i) for i in range(sections - 1)]
    up = [(i, i + 1) for i in range(blocks - 1)]
    down = [(i + 1, i) for i in range(blocks - 1)]
    right = lax.ppermute(right_out.reshape(terms, *square), "sec", ahead)
    state = start_state.reshape(square)
    p0, h0 = call(init_body, [(square, F32), (square, BF)], (live, state), [SM, VM])

    def halo(h):
        return lax.ppermute(h, "blk", up), h, lax.ppermute(h, "blk", down)

    triple = [(square, F32), (square, F32), (square, BF)]
    slots = [pltpu.VMEM((3, *square), BF)]
    inner, total = call(
        inner_body,
        [((terms, *square), BF), (square, F32)],
        (shift, left, *halo(h0), onsite),
        [SM] + [VM] * 5,
        slots,
    )
    w0, p1, h1 = call(outer_body, triple, (live, inner, right, total, p0), [SM] + [VM] * 4)

    def both(h, p):
        args = (shift, live, left, right, *halo(h), onsite, p)
        return call(both_body, triple, args, [SM, SM] + [VM] * 7, slots)

    w1, p2, h2 = both(h1, p1)
    w2, p3, _ = both(h2, p2)
    (gram,) = call(gram_body, [((blocks, 128), F32)], (p0, w0, w1, w2), [VM] * 4)
    parts = lax.all_to_all(gram, "blk", 0, 0, tiled=True)
    theta, half, energy = call(
        final_body, [(square, F32), (square, BF), ((1, 128), F32)], (parts, p0, p1, p2, p3), [VM] * 5
    )
    beside = lax.ppermute(half, "sec", ahead)
    keep = (jnp.arange(width, dtype=jnp.int32) < rank[0, 0]).astype(BF)
    own_part = dot_t(half * keep[None, :], half)
    other_part = lax.dot_general(
        beside * keep[:, None], beside, (((0,), (0,)), ((), ())), preferred_element_type=F32
    )
    density = own_part + other_part
    return theta[None, None], energy[0, :1], density[None, None]


def solution(mesh):
    placed = (
        P("sec", None, "blk", None, None),
        P("sec", None, "blk", None, None),
        P("sec", "blk", None, None),
        P("sec", "blk", None, None),
        P("sec", "blk"),
        P("sec", "blk"),
        P(),
    )
    return jax.shard_map(
        per_device,
        mesh=mesh,
        in_specs=placed,
        out_specs=(P("sec", "blk", None, None), P("sec"), P("sec", "blk", None, None)),
        check_vma=False,
    )
```

```python
import jax
import jax.numpy as jnp
from jax import lax
from jax.experimental import pallas as pl
from jax.experimental.pallas import tpu as pltpu
from jax.sharding import PartitionSpec as P


STEP = 0.3
VM = pl.BlockSpec(memory_space=pltpu.VMEM)
SM = pl.BlockSpec(memory_space=pltpu.SMEM)
F32 = jnp.float32
BF = jnp.bfloat16
LIMIT = 20 * 1024 * 1024


def call(body, outs, args, specs, scratch=(), flops=10**8, out_specs=None):
    moved = sum(a.size * a.dtype.itemsize for a in args)
    return pl.pallas_call(
        body,
        out_shape=[jax.ShapeDtypeStruct(s, d) for s, d in outs],
        in_specs=specs,
        out_specs=out_specs or [VM] * len(outs),
        scratch_shapes=list(scratch),
        compiler_params=pltpu.CompilerParams(vmem_limit_bytes=LIMIT),
        cost_estimate=pl.CostEstimate(flops=flops, bytes_accessed=moved, transcendentals=0),
    )(*args)


def dot(a, b):
    return jnp.dot(a, b, preferred_element_type=F32)


def dot_t(a, b):
    return lax.dot_general(a, b, (((1,), (1,)), ((), ())), preferred_element_type=F32)


def inside(live, shape):
    rows = lax.broadcasted_iota(jnp.int32, shape, 0)
    cols = lax.broadcasted_iota(jnp.int32, shape, 1)
    return (rows < live) & (cols < live)


def init_body(live, start, p_ref, h_ref):
    p = jnp.where(inside(live[0, 0], start.shape), start[...], 0.0)
    p_ref[...] = p
    h_ref[...] = p.astype(BF)


def fill(hs, own, near, far):
    hs[0] = own[...]
    hs[1] = near[...]
    hs[2] = far[...]


def inner_body(slot, left, own, near, far, onsite, inner, total, hs):
    fill(hs, own, near, far)
    h = own[...]
    total[...] = dot(onsite[...], h) + dot_t(h, onsite[...])
    for k in range(left.shape[0]):
        inner[k] = dot(left[k], hs[slot[k]]).astype(BF)


def finish(total, live, p, w_ref, p_ref, h_ref):
    w = jnp.where(inside(live, total.shape), total[...], 0.0)
    w_ref[...] = w
    q = p - STEP * w
    p_ref[...] = q
    h_ref[...] = q.astype(BF)


def outer_sum(inner, right, start):
    total = start[...]
    for k in range(right.shape[0]):
        total = total + dot_t(inner[k], right[k])
    return total


def load_body(left_hbm, onsite_hbm, left, onsite, sem):
    copies = [
        pltpu.make_async_copy(left_hbm, left, sem.at[0]),
        pltpu.make_async_copy(onsite_hbm, onsite, sem.at[1]),
    ]
    for copy in copies:
        copy.start()
    for copy in copies:
        copy.wait()


def even_body(slot, live, inner, right_hbm, start, p, w_ref, p_ref, h_ref, right, sem):
    @pl.when(slot[right.shape[0]] == 0)
    def _():
        terms = right.shape[0]
        copies = [pltpu.make_async_copy(right_hbm.at[k], right.at[k], sem.at[k]) for k in range(terms)]
        for copy in copies:
            copy.start()
        total = start[...]
        for k in range(terms):
            copies[k].wait()
            total = total + dot_t(inner[k], right[k])
        finish(total, live[0, 0], p[...], w_ref, p_ref, h_ref)


def odd_body(slot, live, inner, right, start, p, _, __, w_ref, p_ref, h_ref):
    @pl.when(slot[right.shape[0]] == 1)
    def _():
        finish(outer_sum(inner, right, start), live[0, 0], p[...], w_ref, p_ref, h_ref)


def product(slot, left, right, own, near, far, onsite, hs):
    fill(hs, own, near, far)
    h = own[...]
    total = dot(onsite[...], h) + dot_t(h, onsite[...])
    for k in range(left.shape[0]):
        part = dot(left[k], hs[slot[k]]).astype(BF)
        total = total + dot_t(part, right[k])
    return total


def both_body(slot, live, left, onsite, *refs):
    sets, (w_ref, p_ref, h_ref, old_w, old_p, hs) = (refs[:6], refs[6:12]), refs[12:]
    for turn, (right, own, near, far, p, w) in enumerate(sets):

        @pl.when(slot[left.shape[0]] == turn)
        def _():
            total = product(slot, left, right, own, near, far, onsite, hs)
            finish(total, live[0, 0], p[...], w_ref, p_ref, h_ref)
            old_w[...] = w[...]
            old_p[...] = p[...]


def put(out, base, pairs):
    lane = lax.broadcasted_iota(jnp.int32, out.shape, 1)
    for i, (x, y) in enumerate(pairs):
        out = jnp.where(lane == base + i, jnp.sum(x * y), out)
    return out


def gram_body(p0, w0, w1, g_ref):
    a, b, c = p0[...], w0[...], w1[...]
    pairs = ((a, a), (a, b), (a, c), (b, b), (b, c), (c, c))
    g_ref[...] = put(jnp.zeros(g_ref.shape, F32), 0, pairs)


def last_body(slot, live, left, right_even, right_odd, own, near, far, onsite, p, p0, w0, w1, g, p_ref, g_ref, hs):
    for turn, right in enumerate((right_even, right_odd)):

        @pl.when(slot[left.shape[0]] == turn)
        def _():
            total = product(slot, left, right, own, near, far, onsite, hs)
            w = jnp.where(inside(live[0, 0], total.shape), total, 0.0)
            p_ref[...] = p[...] - STEP * w
            g_ref[...] = put(g[...], 6, ((p0[...], w), (w0[...], w), (w1[...], w), (w, w)))


def coef_body(parts, p0, p1, p2, p3, half_ref, coef_ref):
    sums = jnp.sum(parts[...], axis=0, keepdims=True)
    v = [sums[:, i : i + 1] for i in range(10)]
    weight, p0w = v[0], [v[1], v[2], v[6]]
    ww = [[v[3], v[4], v[7]], [v[4], v[5], v[8]], [v[7], v[8], v[9]]]
    p1w = [p0w[j] - STEP * ww[0][j] for j in range(3)]
    p2w = [p1w[j] - STEP * ww[1][j] for j in range(3)]
    pw = [p0w, p1w, p2w]
    one = jnp.ones_like(weight)
    coef, scale = [one], one
    energy = one
    for n in range(3):
        c = jnp.zeros_like(one)
        a = jnp.zeros_like(one)
        for i in range(n + 1):
            for j in range(n + 1):
                t = coef[i] * coef[j]
                c = c + t * pw[i][j]
                a = a + t * ww[i][j]
        energy = c * scale / weight
        excess = jnp.maximum(a * scale / weight - energy * energy, 0.0)
        scale = scale / (1.0 + STEP * STEP * excess)
        g = STEP * energy
        coef = [g * coef[0]] + [coef[i - 1] + g * coef[i] for i in range(1, n + 1)] + [one]
    root = jnp.sqrt(scale)
    coef = [root * c for c in coef]
    theta = coef[0] * p0[...] + coef[1] * p1[...] + coef[2] * p2[...] + coef[3] * p3[...]
    half_ref[...] = theta.astype(BF)
    row = lax.broadcasted_iota(jnp.int32, coef_ref.shape, 0)
    out = jnp.broadcast_to(energy, coef_ref.shape)
    for i, c in enumerate(coef):
        out = jnp.where(row == i, c, out)
    coef_ref[...] = out


def theta_body(coef, p0, p1, p2, p3, theta_ref):
    c = [coef[i : i + 1, 0:1] for i in range(4)]
    theta_ref[...] = c[0] * p0[...] + c[1] * p1[...] + c[2] * p2[...] + c[3] * p3[...]


def own_body(rank, half, own_ref):
    h = half[...]
    cols = lax.broadcasted_iota(jnp.int32, h.shape, 1)
    own_ref[...] = dot_t(jnp.where(cols < rank[0, 0], h, jnp.zeros_like(h)), h)


def density_body(rank, beside, own, out_ref):
    b = beside[...]
    rows = lax.broadcasted_iota(jnp.int32, b.shape, 0)
    kept = jnp.where(rows < rank[0, 0], b, jnp.zeros_like(b))
    other = lax.dot_general(kept, b, (((0,), (0,)), ((), ())), preferred_element_type=F32)
    out_ref[...] = own[...] + other


def section_step(left_env, right_out, onsite, start_state, live, rank, shift):
    terms, width = left_env.shape[1], left_env.shape[-1]
    square = (width, width)
    left = left_env.reshape(terms, *square)
    onsite = onsite.reshape(square)
    sections, blocks = lax.axis_size("sec"), lax.axis_size("blk")
    sec, blk = lax.axis_index("sec"), lax.axis_index("blk")
    ahead = [(i + 1, i) for i in range(sections - 1)]
    near_pairs = [(i, i ^ 1) for i in range(blocks) if i ^ 1 < blocks]
    far_pairs = [(i, (i - 1 ^ 1) + 1) for i in range(1, blocks) if (i - 1 ^ 1) + 1 < blocks]
    near_shift = 1 - 2 * (blk % 2)
    slot = jnp.where(shift == 0, 0, jnp.where(shift == near_shift, 1, 2)).astype(jnp.int32)
    slot = jnp.concatenate([slot, jnp.full((1,), sec % 2, jnp.int32)])
    built = right_out.reshape(terms, *square)
    right_odd = lax.ppermute(built, "sec", ahead[1::2])
    state = start_state.reshape(square)
    p0, h0 = call(init_body, [(square, F32), (square, BF)], (live, state), [SM, VM])
    hbm = pl.BlockSpec(memory_space=pl.ANY)
    outs = [((terms, *square), BF), (square, BF)]
    sems = [pltpu.SemaphoreType.DMA((2,))]
    left, onsite = call(load_body, outs, (left, onsite), [hbm, hbm], sems)

    def halo(h, which):
        def pairs(base):
            return [(s * blocks + i, s * blocks + j) for s in which for i, j in base]

        axes = ("sec", "blk")
        near = lax.ppermute(h, axes, pairs(near_pairs))
        far = lax.ppermute(h, axes, pairs(far_pairs))
        return near, far

    every = range(sections)
    triple = [(square, F32), (square, F32), (square, BF)]
    slots = [pltpu.VMEM((3, *square), BF)]
    near, far = halo(h0, every)
    right_even = lax.ppermute(built, "sec", ahead[0::2])
    inner, total = call(
        inner_body,
        [((terms, *square), BF), (square, F32)],
        (slot, left, h0, near, far, onsite),
        [SM] + [VM] * 5,
        slots,
    )
    args = (slot, live, inner, right_even, total, p0)
    specs = [SM, SM, VM, hbm, VM, VM]
    outs = triple + [((terms, *square), BF)]
    w0, p1, h1, right_even = call(even_body, outs, args, specs, [pltpu.SemaphoreType.DMA((terms,))])
    near, far = halo(h1, every[0::2])
    sets = [right_even, h1, near, far, p1, w0]
    args = (slot, live, inner, right_odd, total, p0, near, far)
    w0, p1, h1 = call(odd_body, triple, args, [SM, SM] + [VM] * 4 + [hbm] * 2)
    sets += [right_odd, h1, *halo(h1, every[1::2]), p1, w0]
    outs = triple + [(square, F32)] * 2
    w1, p2, h2, w0, p1 = call(both_body, outs, (slot, live, left, onsite, *sets), [SM, SM] + [VM] * 14, slots)
    table = (blocks, 128)
    (gram,) = call(gram_body, [(table, F32)], (p0, w0, w1), [VM] * 3)
    args = (slot, live, left, right_even, right_odd, h2, *halo(h2, every), onsite, p2, p0, w0, w1, gram)
    p3, gram = call(last_body, [(square, F32), (table, F32)], args, [SM, SM] + [VM] * 12, slots)
    parts = lax.all_to_all(gram, "blk", 0, 0, tiled=True)
    half, coef = call(coef_body, [(square, BF), ((8, 128), F32)], (parts, p0, p1, p2, p3), [VM] * 5)
    beside = lax.ppermute(half, "sec", ahead)
    (theta,) = call(theta_body, [(square, F32)], (coef, p0, p1, p2, p3), [VM] * 5)
    (own,) = call(own_body, [(square, F32)], (rank, half), [SM, VM])
    (density,) = call(density_body, [(square, F32)], (rank, beside, own), [SM, VM, VM])
    return theta[None, None], coef[4, :1], density[None, None]


def solution(mesh):
    placed = (
        P("sec", None, "blk", None, None),
        P("sec", None, "blk", None, None),
        P("sec", "blk", None, None),
        P("sec", "blk", None, None),
        P("sec", "blk"),
        P("sec", "blk"),
        P(),
    )
    return jax.shard_map(
        section_step,
        mesh=mesh,
        in_specs=placed,
        out_specs=(P("sec", "blk", None, None), P("sec"), P("sec", "blk", None, None)),
        check_vma=False,
    )
```

```python
import jax
import jax.numpy as jnp
from jax import lax
from jax.experimental import pallas as pl
from jax.experimental.pallas import tpu as pltpu
from jax.sharding import PartitionSpec as P


STEP = 0.3
PARITY_BIT = 30
VM = pl.BlockSpec(memory_space=pltpu.VMEM)
SM = pl.BlockSpec(memory_space=pltpu.SMEM)
F32 = jnp.float32
BF = jnp.bfloat16
LIMIT = 20 * 1024 * 1024


def call(body, outs, args, specs, scratch=(), flops=10**8, out_specs=None):
    moved = sum(a.size * a.dtype.itemsize for a in args)
    return pl.pallas_call(
        body,
        out_shape=[jax.ShapeDtypeStruct(s, d) for s, d in outs],
        in_specs=specs,
        out_specs=out_specs or [VM] * len(outs),
        scratch_shapes=list(scratch),
        compiler_params=pltpu.CompilerParams(vmem_limit_bytes=LIMIT),
        cost_estimate=pl.CostEstimate(flops=flops, bytes_accessed=moved, transcendentals=0),
    )(*args)


def dot(a, b):
    return jnp.dot(a, b, preferred_element_type=F32)


def dot_t(a, b):
    return lax.dot_general(a, b, (((1,), (1,)), ((), ())), preferred_element_type=F32)


def inside(live, shape):
    rows = lax.broadcasted_iota(jnp.int32, shape, 0)
    cols = lax.broadcasted_iota(jnp.int32, shape, 1)
    return (rows < live) & (cols < live)


def init_body(live, start, p_ref, h_ref):
    p = jnp.where(inside(live[0, 0], start.shape), start[...], 0.0)
    p_ref[...] = p
    h_ref[...] = p.astype(BF)


def slot_of(code, k):
    return lax.bitwise_and(lax.shift_right_logical(code[0, 0], jnp.int32(2 * k)), jnp.int32(3))


def parity(code):
    return lax.bitwise_and(lax.shift_right_logical(code[0, 0], jnp.int32(PARITY_BIT)), jnp.int32(1))


def fill(hs, own, near, far):
    hs[0] = own[...]
    hs[1] = near[...]
    hs[2] = far[...]


def inner_body(slot, left, own, near, far, onsite, inner, total, hs):
    fill(hs, own, near, far)
    h = own[...]
    total[...] = dot(onsite[...], h) + dot_t(h, onsite[...])
    for k in range(left.shape[0]):
        inner[k] = dot(left[k], hs[slot_of(slot, k)]).astype(BF)


def finish(total, live, p, w_ref, p_ref, h_ref):
    w = jnp.where(inside(live, total.shape), total[...], 0.0)
    w_ref[...] = w
    q = p - STEP * w
    p_ref[...] = q
    h_ref[...] = q.astype(BF)


def outer_sum(inner, right, start):
    total = start[...]
    for k in range(right.shape[0]):
        total = total + dot_t(inner[k], right[k])
    return total


def load_body(left_hbm, onsite_hbm, left, onsite, sem):
    copies = [
        pltpu.make_async_copy(left_hbm, left, sem.at[0]),
        pltpu.make_async_copy(onsite_hbm, onsite, sem.at[1]),
    ]
    for copy in copies:
        copy.start()
    for copy in copies:
        copy.wait()


def even_body(slot, live, inner, right_hbm, start, p, w_ref, p_ref, h_ref, right, sem):
    @pl.when(parity(slot) == 0)
    def _():
        half = right.shape[0] // 2
        copies = [
            pltpu.make_async_copy(right_hbm.at[:half], right.at[:half], sem.at[0]),
            pltpu.make_async_copy(right_hbm.at[half:], right.at[half:], sem.at[1]),
        ]
        for copy in copies:
            copy.start()
        total = start[...]
        for k in range(right.shape[0]):
            if k in (0, half):
                copies[k // half].wait()
            total = total + dot_t(inner[k], right[k])
        finish(total, live[0, 0], p[...], w_ref, p_ref, h_ref)


def odd_body(live, inner, right, start, p, _, __, w_ref, p_ref, h_ref):
    finish(outer_sum(inner, right, start), live[0, 0], p[...], w_ref, p_ref, h_ref)


def product(slot, left, right, own, near, far, onsite, hs):
    fill(hs, own, near, far)
    h = own[...]
    total = dot(onsite[...], h) + dot_t(h, onsite[...])
    for k in range(left.shape[0]):
        part = dot(left[k], hs[slot_of(slot, k)]).astype(BF)
        total = total + dot_t(part, right[k])
    return total


def both_body(slot, live, left, onsite, *refs):
    sets, (w_ref, p_ref, h_ref, old_w, old_p, hs) = (refs[:6], refs[6:12]), refs[12:]
    for turn, (right, own, near, far, p, w) in enumerate(sets):

        @pl.when(parity(slot) == turn)
        def _():
            total = product(slot, left, right, own, near, far, onsite, hs)
            finish(total, live[0, 0], p[...], w_ref, p_ref, h_ref)
            old_w[...] = w[...]
            old_p[...] = p[...]


def put(out, base, pairs):
    lane = lax.broadcasted_iota(jnp.int32, out.shape, 1)
    for i, (x, y) in enumerate(pairs):
        out = jnp.where(lane == base + i, jnp.sum(x * y), out)
    return out


def gram_body(p0, w0, w1, g_ref):
    a, b, c = p0[...], w0[...], w1[...]
    pairs = ((a, a), (a, b), (a, c), (b, b), (b, c), (c, c))
    g_ref[...] = put(jnp.zeros(g_ref.shape, F32), 0, pairs)


def last_body(slot, live, left, right_even, right_odd, own, near, far, onsite, p, p0, w0, w1, g, p_ref, g_ref, hs):
    for turn, right in enumerate((right_even, right_odd)):

        @pl.when(parity(slot) == turn)
        def _():
            total = product(slot, left, right, own, near, far, onsite, hs)
            w = jnp.where(inside(live[0, 0], total.shape), total, 0.0)
            p_ref[...] = p[...] - STEP * w
            g_ref[...] = put(g[...], 6, ((p0[...], w), (w0[...], w), (w1[...], w), (w, w)))


def coefficients(parts, p0, p1, p2, p3, half_ref, coef_ref):
    sums = jnp.sum(parts[...], axis=0, keepdims=True)
    v = [sums[:, i : i + 1] for i in range(10)]
    weight, p0w = v[0], [v[1], v[2], v[6]]
    ww = [[v[3], v[4], v[7]], [v[4], v[5], v[8]], [v[7], v[8], v[9]]]
    p1w = [p0w[j] - STEP * ww[0][j] for j in range(3)]
    p2w = [p1w[j] - STEP * ww[1][j] for j in range(3)]
    pw = [p0w, p1w, p2w]
    one = jnp.ones_like(weight)
    coef, scale, inverse = [one], one, 1.0 / weight
    energy = one
    for n in range(3):
        c = jnp.zeros_like(one)
        a = jnp.zeros_like(one)
        for i in range(n + 1):
            for j in range(n + 1):
                t = coef[i] * coef[j]
                c = c + t * pw[i][j]
                a = a + t * ww[i][j]
        energy = c * scale * inverse
        excess = jnp.maximum(a * scale * inverse - energy * energy, 0.0)
        scale = scale / (1.0 + STEP * STEP * excess)
        g = STEP * energy
        coef = [g * coef[0]] + [coef[i - 1] + g * coef[i] for i in range(1, n + 1)] + [one]
    root = jnp.sqrt(scale)
    coef = [root * c for c in coef]
    theta = coef[0] * p0[...] + coef[1] * p1[...] + coef[2] * p2[...] + coef[3] * p3[...]
    half_ref[...] = theta.astype(BF)
    row = lax.broadcasted_iota(jnp.int32, coef_ref.shape, 0)
    out = jnp.broadcast_to(energy, coef_ref.shape)
    for i, c in enumerate(coef):
        out = jnp.where(row == i, c, out)
    coef_ref[...] = out


def coef_even_body(slot, *refs):
    @pl.when(parity(slot) == 0)
    def _():
        coefficients(*refs)


def coef_odd_body(slot, half_even, coef_even, parts, p0, p1, p2, p3, half_ref, coef_ref):
    odd = parity(slot) == 1

    @pl.when(odd)
    def _():
        coefficients(parts, p0, p1, p2, p3, half_ref, coef_ref)

    @pl.when(jnp.logical_not(odd))
    def _():
        half_ref[...] = half_even[...]
        coef_ref[...] = coef_even[...]


def theta_body(coef, p0, p1, p2, p3, theta_ref):
    c = [coef[i : i + 1, 0:1] for i in range(4)]
    theta_ref[...] = c[0] * p0[...] + c[1] * p1[...] + c[2] * p2[...] + c[3] * p3[...]


def own_body(rank, half, own_ref):
    h = half[...]
    cols = lax.broadcasted_iota(jnp.int32, h.shape, 1)
    own_ref[...] = dot_t(jnp.where(cols < rank[0, 0], h, jnp.zeros_like(h)), h)


def density_body(slot, rank, beside, beside_odd, own, out_hbm, out, sem):
    b = jnp.where(parity(slot) == 1, beside_odd[...], beside[...])
    rows = lax.broadcasted_iota(jnp.int32, b.shape, 0)
    kept = jnp.where(rows < rank[0, 0], b, jnp.zeros_like(b))
    half = b.shape[0] // 2
    copies = []
    for i in range(2):
        part = pl.ds(i * half, half)
        columns = kept[:, i * half : (i + 1) * half]
        other = lax.dot_general(columns, b, (((0,), (0,)), ((), ())), preferred_element_type=F32)
        out[part] = own[part] + other
        copies.append(pltpu.make_async_copy(out.at[part], out_hbm.at[part], sem.at[i]))
        copies[i].start()
    for copy in copies:
        copy.wait()


def section_step(left_env, right_out, onsite, start_state, live, rank, shift):
    terms, width = left_env.shape[1], left_env.shape[-1]
    square = (width, width)
    left = left_env.reshape(terms, *square)
    onsite = onsite.reshape(square)
    sections, blocks = lax.axis_size("sec"), lax.axis_size("blk")
    sec, blk = lax.axis_index("sec"), lax.axis_index("blk")
    ahead = [(i + 1, i) for i in range(sections - 1)]
    near_pairs = [(i, i ^ 1) for i in range(blocks) if i ^ 1 < blocks]
    far_pairs = [(i, (i - 1 ^ 1) + 1) for i in range(1, blocks) if (i - 1 ^ 1) + 1 < blocks]
    near_shift = 1 - 2 * (blk % 2)
    slot = jnp.where(shift == 0, 0, jnp.where(shift == near_shift, 1, 2)).astype(jnp.int32)
    assert 2 * terms <= PARITY_BIT
    code = jnp.sum(slot << (2 * jnp.arange(terms, dtype=jnp.int32))) + ((sec % 2) << PARITY_BIT)
    slot = code.astype(jnp.int32).reshape(1, 1)
    built = right_out.reshape(terms, *square)
    right_odd = lax.ppermute(built, "sec", ahead[1::2])
    state = start_state.reshape(square)
    p0, h0 = call(init_body, [(square, F32), (square, BF)], (live, state), [SM, VM])
    hbm = pl.BlockSpec(memory_space=pl.ANY)
    outs = [((terms, *square), BF), (square, BF)]
    sems = [pltpu.SemaphoreType.DMA((2,))]
    left, onsite = call(load_body, outs, (left, onsite), [hbm, hbm], sems)

    def halo(h, which):
        def pairs(base):
            return [(s * blocks + i, s * blocks + j) for s in which for i, j in base]

        axes = ("sec", "blk")
        near = lax.ppermute(h, axes, pairs(near_pairs))
        far = lax.ppermute(h, axes, pairs(far_pairs))
        return near, far

    every = range(sections)
    triple = [(square, F32), (square, F32), (square, BF)]
    slots = [pltpu.VMEM((3, *square), BF)]
    near, far = halo(h0, every)
    right_even = lax.ppermute(built, "sec", ahead[0::2])
    inner, total = call(
        inner_body,
        [((terms, *square), BF), (square, F32)],
        (slot, left, h0, near, far, onsite),
        [SM] + [VM] * 5,
        slots,
    )
    args = (slot, live, inner, right_even, total, p0)
    specs = [SM, SM, VM, hbm, VM, VM]
    outs = triple + [((terms, *square), BF)]
    w0, p1, h1, right_even = call(even_body, outs, args, specs, [pltpu.SemaphoreType.DMA((2,))])
    near, far = halo(h1, every[0::2])
    sets = [right_even, h1, near, far, p1, w0]
    args = (live, inner, right_odd, total, p0, near, far)
    w0, p1, h1 = call(odd_body, triple, args, [SM] + [VM] * 4 + [hbm] * 2)
    sets += [right_odd, h1, *halo(h1, every[1::2]), p1, w0]
    outs = triple + [(square, F32)] * 2
    w1, p2, h2, w0, p1 = call(both_body, outs, (slot, live, left, onsite, *sets), [SM, SM] + [VM] * 14, slots)
    table = (blocks, 128)
    (gram,) = call(gram_body, [(table, F32)], (p0, w0, w1), [VM] * 3)
    args = (slot, live, left, right_even, right_odd, h2, *halo(h2, every), onsite, p2, p0, w0, w1, gram)
    p3, gram = call(last_body, [(square, F32), (table, F32)], args, [SM, SM] + [VM] * 12, slots)
    parts = lax.all_to_all(gram, "blk", 0, 0, tiled=True)
    outs = [(square, BF), ((8, 128), F32)]
    args = (parts, p0, p1, p2, p3)
    half, coef = call(coef_even_body, outs, (slot, *args), [SM] + [VM] * 5)
    beside_odd = lax.ppermute(half, "sec", ahead[1::2])
    half, coef = call(coef_odd_body, outs, (slot, half, coef, *args), [SM] + [VM] * 7)
    beside = lax.ppermute(half, "sec", ahead[0::2])
    (theta,) = call(theta_body, [(square, F32)], (coef, p0, p1, p2, p3), [VM] * 5)
    (own,) = call(own_body, [(square, F32)], (rank, half), [SM, VM])
    scratch = [pltpu.VMEM(square, F32), pltpu.SemaphoreType.DMA((2,))]
    args = (slot, rank, beside, beside_odd, own)
    (density,) = call(density_body, [(square, F32)], args, [SM, SM] + [VM] * 3, scratch, out_specs=[hbm])
    return theta[None, None], coef[4, :1], density[None, None]


def solution(mesh):
    placed = (
        P("sec", None, "blk", None, None),
        P("sec", None, "blk", None, None),
        P("sec", "blk", None, None),
        P("sec", "blk", None, None),
        P("sec", "blk"),
        P("sec", "blk"),
        P(),
    )
    return jax.shard_map(
        section_step,
        mesh=mesh,
        in_specs=placed,
        out_specs=(P("sec", "blk", None, None), P("sec"), P("sec", "blk", None, None)),
        check_vma=False,
    )
```

```python
import jax
import jax.numpy as jnp
from jax import lax
from jax.experimental import pallas as pl
from jax.experimental.pallas import tpu as pltpu
from jax.sharding import PartitionSpec as P


STEP = 0.3
PARITY_BIT = 30
VM = pl.BlockSpec(memory_space=pltpu.VMEM)
SM = pl.BlockSpec(memory_space=pltpu.SMEM)
F32 = jnp.float32
BF = jnp.bfloat16
LIMIT = 20 * 1024 * 1024


def call(body, outs, args, specs, scratch=(), flops=10**8, out_specs=None):
    moved = sum(a.size * a.dtype.itemsize for a in args)
    return pl.pallas_call(
        body,
        out_shape=[jax.ShapeDtypeStruct(s, d) for s, d in outs],
        in_specs=specs,
        out_specs=out_specs or [VM] * len(outs),
        scratch_shapes=list(scratch),
        compiler_params=pltpu.CompilerParams(vmem_limit_bytes=LIMIT),
        cost_estimate=pl.CostEstimate(flops=flops, bytes_accessed=moved, transcendentals=0),
    )(*args)


def dot(a, b):
    return jnp.dot(a, b, preferred_element_type=F32)


def dot_t(a, b):
    return lax.dot_general(a, b, (((1,), (1,)), ((), ())), preferred_element_type=F32)


def inside(live, shape):
    rows = lax.broadcasted_iota(jnp.int32, shape, 0)
    cols = lax.broadcasted_iota(jnp.int32, shape, 1)
    return (rows < live) & (cols < live)


def init_body(live, start, p_ref, h_ref):
    p = jnp.where(inside(live[0, 0], start.shape), start[...], 0.0)
    p_ref[...] = p
    h_ref[...] = p.astype(BF)


def slot_of(code, k):
    return lax.bitwise_and(lax.shift_right_logical(code[0, 0], jnp.int32(2 * k)), jnp.int32(3))


def parity(code):
    return lax.bitwise_and(lax.shift_right_logical(code[0, 0], jnp.int32(PARITY_BIT)), jnp.int32(1))


def fill(hs, own, near, far):
    hs[0] = own[...]
    hs[1] = near[...]
    hs[2] = far[...]


def inner_body(slot, left, own, near, far, onsite, inner, total, hs):
    fill(hs, own, near, far)
    h = own[...]
    total[...] = dot(onsite[...], h) + dot_t(h, onsite[...])
    for k in range(left.shape[0]):
        inner[k] = dot(left[k], hs[slot_of(slot, k)]).astype(BF)


def finish(total, live, p, w_ref, p_ref, h_ref):
    w = jnp.where(inside(live, total.shape), total[...], 0.0)
    w_ref[...] = w
    q = p - STEP * w
    p_ref[...] = q
    h_ref[...] = q.astype(BF)


def outer_sum(inner, right, start):
    total = start[...]
    for k in range(right.shape[0]):
        total = total + dot_t(inner[k], right[k])
    return total


def load_body(left_hbm, onsite_hbm, left, onsite, sem):
    copies = [
        pltpu.make_async_copy(left_hbm, left, sem.at[0]),
        pltpu.make_async_copy(onsite_hbm, onsite, sem.at[1]),
    ]
    for copy in copies:
        copy.start()
    for copy in copies:
        copy.wait()


def even_body(slot, live, inner, right_hbm, start, p, w_ref, p_ref, h_ref, right, sem):
    @pl.when(parity(slot) == 0)
    def _():
        half = right.shape[0] // 2
        copies = [
            pltpu.make_async_copy(right_hbm.at[:half], right.at[:half], sem.at[0]),
            pltpu.make_async_copy(right_hbm.at[half:], right.at[half:], sem.at[1]),
        ]
        for copy in copies:
            copy.start()
        total = start[...]
        for k in range(right.shape[0]):
            if k in (0, half):
                copies[k // half].wait()
            total = total + dot_t(inner[k], right[k])
        finish(total, live[0, 0], p[...], w_ref, p_ref, h_ref)


def odd_body(slot, live, inner, right, start, p, _, __, w_ref, p_ref, h_ref):
    @pl.when(parity(slot) == 1)
    def _():
        finish(outer_sum(inner, right, start), live[0, 0], p[...], w_ref, p_ref, h_ref)


def product(slot, left, right, own, near, far, onsite, hs):
    fill(hs, own, near, far)
    h = own[...]
    total = dot(onsite[...], h) + dot_t(h, onsite[...])
    for k in range(left.shape[0]):
        part = dot(left[k], hs[slot_of(slot, k)]).astype(BF)
        total = total + dot_t(part, right[k])
    return total


def both_body(slot, live, left, onsite, *refs):
    sets, (w_ref, p_ref, h_ref, old_w, old_p, hs) = (refs[:6], refs[6:12]), refs[12:]
    for turn, (right, own, near, far, p, w) in enumerate(sets):

        @pl.when(parity(slot) == turn)
        def _():
            total = product(slot, left, right, own, near, far, onsite, hs)
            finish(total, live[0, 0], p[...], w_ref, p_ref, h_ref)
            old_w[...] = w[...]
            old_p[...] = p[...]


def put(out, base, pairs):
    lane = lax.broadcasted_iota(jnp.int32, out.shape, 1)
    for i, (x, y) in enumerate(pairs):
        out = jnp.where(lane == base + i, jnp.sum(x * y), out)
    return out


def gram_body(_, p0, w0, w1, g_ref):
    a, b, c = p0[...], w0[...], w1[...]
    pairs = ((a, a), (a, b), (a, c), (b, b), (b, c), (c, c))
    g_ref[...] = put(jnp.zeros(g_ref.shape, F32), 0, pairs)


def last_body(slot, live, left, right_even, right_odd, own, near, far, onsite, p, p0, w0, w1, g, p_ref, g_ref, hs):
    for turn, right in enumerate((right_even, right_odd)):

        @pl.when(parity(slot) == turn)
        def _():
            total = product(slot, left, right, own, near, far, onsite, hs)
            w = jnp.where(inside(live[0, 0], total.shape), total, 0.0)
            p_ref[...] = p[...] - STEP * w
            g_ref[...] = put(g[...], 6, ((p0[...], w), (w0[...], w), (w1[...], w), (w, w)))


def coefficients(parts, p0, p1, p2, p3, half_ref, coef_ref):
    sums = jnp.sum(parts[...], axis=0, keepdims=True)
    v = [sums[:, i : i + 1] for i in range(10)]
    weight, p0w = v[0], [v[1], v[2], v[6]]
    ww = [[v[3], v[4], v[7]], [v[4], v[5], v[8]], [v[7], v[8], v[9]]]
    p1w = [p0w[j] - STEP * ww[0][j] for j in range(3)]
    p2w = [p1w[j] - STEP * ww[1][j] for j in range(3)]
    pw = [p0w, p1w, p2w]
    one = jnp.ones_like(weight)
    coef, scale, inverse = [one], one, 1.0 / weight
    energy = one
    for n in range(3):
        c = jnp.zeros_like(one)
        a = jnp.zeros_like(one)
        for i in range(n + 1):
            for j in range(n + 1):
                t = coef[i] * coef[j]
                c = c + t * pw[i][j]
                a = a + t * ww[i][j]
        energy = c * scale * inverse
        excess = jnp.maximum(a * scale * inverse - energy * energy, 0.0)
        scale = scale / (1.0 + STEP * STEP * excess)
        g = STEP * energy
        coef = [g * coef[0]] + [coef[i - 1] + g * coef[i] for i in range(1, n + 1)] + [one]
    root = jnp.sqrt(scale)
    coef = [root * c for c in coef]
    theta = coef[0] * p0[...] + coef[1] * p1[...] + coef[2] * p2[...] + coef[3] * p3[...]
    half_ref[...] = theta.astype(BF)
    row = lax.broadcasted_iota(jnp.int32, coef_ref.shape, 0)
    out = jnp.broadcast_to(energy, coef_ref.shape)
    for i, c in enumerate(coef):
        out = jnp.where(row == i, c, out)
    coef_ref[...] = out


def coef_even_body(slot, *refs):
    @pl.when(parity(slot) == 0)
    def _():
        coefficients(*refs)


def coef_odd_body(slot, half_even, coef_even, parts, p0, p1, p2, p3, half_ref, coef_ref):
    odd = parity(slot) == 1

    @pl.when(odd)
    def _():
        coefficients(parts, p0, p1, p2, p3, half_ref, coef_ref)

    @pl.when(jnp.logical_not(odd))
    def _():
        half_ref[...] = half_even[...]
        coef_ref[...] = coef_even[...]


def theta_body(coef, p0, p1, p2, p3, theta_ref, energy_ref):
    c = [coef[i : i + 1, 0:1] for i in range(4)]
    theta_ref[...] = c[0] * p0[...] + c[1] * p1[...] + c[2] * p2[...] + c[3] * p3[...]
    energy_ref[...] = coef[4:5, 0:1]


def own_body(rank, half, own_ref):
    h = half[...]
    cols = lax.broadcasted_iota(jnp.int32, h.shape, 1)
    own_ref[...] = dot_t(jnp.where(cols < rank[0, 0], h, jnp.zeros_like(h)), h)


def density_body(slot, rank, beside, beside_odd, own, out_hbm, out, sem):
    b = jnp.where(parity(slot) == 1, beside_odd[...], beside[...])
    rows = lax.broadcasted_iota(jnp.int32, b.shape, 0)
    kept = jnp.where(rows < rank[0, 0], b, jnp.zeros_like(b))
    half = b.shape[0] // 2
    copies = []
    for i in range(2):
        part = pl.ds(i * half, half)
        columns = kept[:, i * half : (i + 1) * half]
        other = lax.dot_general(columns, b, (((0,), (0,)), ((), ())), preferred_element_type=F32)
        out[part] = own[part] + other
        copies.append(pltpu.make_async_copy(out.at[part], out_hbm.at[part], sem.at[i]))
        copies[i].start()
    for copy in copies:
        copy.wait()


def section_step(left_env, right_out, onsite, start_state, live, rank, shift):
    terms, width = left_env.shape[1], left_env.shape[-1]
    square = (width, width)
    left = left_env.reshape(terms, *square)
    onsite = onsite.reshape(square)
    sections, blocks = lax.axis_size("sec"), lax.axis_size("blk")
    sec, blk = lax.axis_index("sec"), lax.axis_index("blk")
    ahead = [(i + 1, i) for i in range(sections - 1)]
    near_pairs = [(i, i ^ 1) for i in range(blocks) if i ^ 1 < blocks]
    far_pairs = [(i, (i - 1 ^ 1) + 1) for i in range(1, blocks) if (i - 1 ^ 1) + 1 < blocks]
    near_shift = 1 - 2 * (blk % 2)
    slot = jnp.where(shift == 0, 0, jnp.where(shift == near_shift, 1, 2)).astype(jnp.int32)
    assert 2 * terms <= PARITY_BIT
    code = jnp.sum(slot << (2 * jnp.arange(terms, dtype=jnp.int32))) + ((sec % 2) << PARITY_BIT)
    slot = code.astype(jnp.int32).reshape(1, 1)
    built = right_out.reshape(terms, *square)
    right_odd = lax.ppermute(built, "sec", ahead[1::2])
    state = start_state.reshape(square)
    p0, h0 = call(init_body, [(square, F32), (square, BF)], (live, state), [SM, VM])
    hbm = pl.BlockSpec(memory_space=pl.ANY)
    outs = [((terms, *square), BF), (square, BF)]
    sems = [pltpu.SemaphoreType.DMA((2,))]
    left, onsite = call(load_body, outs, (left, onsite), [hbm, hbm], sems)

    def halo(h, which):
        def pairs(base):
            return [(s * blocks + i, s * blocks + j) for s in which for i, j in base]

        axes = ("sec", "blk")
        near = lax.ppermute(h, axes, pairs(near_pairs))
        far = lax.ppermute(h, axes, pairs(far_pairs))
        return near, far

    every = range(sections)
    triple = [(square, F32), (square, F32), (square, BF)]
    slots = [pltpu.VMEM((3, *square), BF)]
    near, far = halo(h0, every)
    right_even = lax.ppermute(built, "sec", ahead[0::2])
    inner, total = call(
        inner_body,
        [((terms, *square), BF), (square, F32)],
        (slot, left, h0, near, far, onsite),
        [SM] + [VM] * 5,
        slots,
    )
    args = (slot, live, inner, right_even, total, p0)
    specs = [SM, SM, VM, hbm, VM, VM]
    outs = triple + [((terms, *square), BF)]
    w0, p1, h1, right_even = call(even_body, outs, args, specs, [pltpu.SemaphoreType.DMA((2,))])
    near, far = halo(h1, every[0::2])
    sets = [right_even, h1, near, far, p1, w0]
    args = (slot, live, inner, right_odd, total, p0, near, far)
    w0, p1, h1 = call(odd_body, triple, args, [SM, SM] + [VM] * 4 + [hbm] * 2)
    sets += [right_odd, h1, *halo(h1, every[1::2]), p1, w0]
    outs = triple + [(square, F32)] * 2
    w1, p2, h2, w0, p1 = call(both_body, outs, (slot, live, left, onsite, *sets), [SM, SM] + [VM] * 14, slots)
    table = (blocks, 128)
    (gram,) = call(gram_body, [(table, F32)], (rank, p0, w0, w1), [SM] + [VM] * 3)
    args = (slot, live, left, right_even, right_odd, h2, *halo(h2, every), onsite, p2, p0, w0, w1, gram)
    p3, gram = call(last_body, [(square, F32), (table, F32)], args, [SM, SM] + [VM] * 12, slots)
    parts = lax.all_to_all(gram, "blk", 0, 0, tiled=True)
    outs = [(square, BF), ((8, 128), F32)]
    args = (parts, p0, p1, p2, p3)
    half, coef = call(coef_even_body, outs, (slot, *args), [SM] + [VM] * 5)
    beside_odd = lax.ppermute(half, "sec", ahead[1::2])
    half, coef = call(coef_odd_body, outs, (slot, half, coef, *args), [SM] + [VM] * 7)
    beside = lax.ppermute(half, "sec", ahead[0::2])
    outs = [(square, F32), ((1, 1), F32)]
    theta, energy = call(theta_body, outs, (coef, p0, p1, p2, p3), [VM] * 5)
    (own,) = call(own_body, [(square, F32)], (rank, half), [SM, VM])
    scratch = [pltpu.VMEM(square, F32), pltpu.SemaphoreType.DMA((2,))]
    args = (slot, rank, beside, beside_odd, own)
    (density,) = call(density_body, [(square, F32)], args, [SM, SM] + [VM] * 3, scratch, out_specs=[hbm])
    return theta[None, None], energy.reshape(1), density[None, None]


def solution(mesh):
    placed = (
        P("sec", None, "blk", None, None),
        P("sec", None, "blk", None, None),
        P("sec", "blk", None, None),
        P("sec", "blk", None, None),
        P("sec", "blk"),
        P("sec", "blk"),
        P(),
    )
    return jax.shard_map(
        section_step,
        mesh=mesh,
        in_specs=placed,
        out_specs=(P("sec", "blk", None, None), P("sec"), P("sec", "blk", None, None)),
        check_vma=False,
    )
```
